1024 devices in a mesh: ctx: 64 (over y_lo, z, core), fsdp: 16 (over y_hi, x).
Axes of the slice: x: 4, y: 8 (y_hi: 4, y_lo: 2; y = y_hi * 2 + y_lo), z: 16, core: 2. Of those that a mesh axis runs over, the one named last changes fastest.
Arguments:
- latents: bfloat16 [16, 8192, 4096], P('fsdp', 'ctx'), may hold values from -6 to 6
- queries: bfloat16 [16, 8192, 2048], P('fsdp', 'ctx')
- values: bfloat16 [16, 8192, 512], P('fsdp', 'ctx'), may hold values from -6 to 6
- d_out: bfloat16 [16, 8192, 2048], P('fsdp', 'ctx'), may hold values from -6 to 6
- w_key: bfloat16 [4096, 512], P('fsdp'), may hold values from -0.09375 to 0.09375
- doc_first: int32 [16, 8192], P('fsdp', 'ctx'), may hold values from 0 to 8191, as said below
Outputs:
- attended: bfloat16 [16, 8192, 2048], P('fsdp', 'ctx')
- grad_query: bfloat16 [16, 8192, 2048], P('fsdp', 'ctx')
- grad_value: bfloat16 [16, 8192, 512], P('fsdp', 'ctx')
- grad_weight: float32 [4096, 512], P('fsdp')
The draws below stay inside these ranges and needn't reach their ends.
Inputs may be any that keep to these rules, and one draw needn't show every extreme that they name: Non-decreasing along each sequence; doc_first[i] <= i, equal to i exactly at a document's first latent, the same for all latents of a document; the first and the last latent of each sequence begin documents.
All inputs are finite; a program needn't handle non-finite values.
Results may differ from the reference program's by a relative error of at most 0.038.
Values may be sent and summed in bfloat16 or wider, within the bound.
No kernel may reach another device: no remote copies, remote signals or barrier semaphores. Data moves between devices by JAX's collectives and lax.ppermute only.
A program may use at most 64 MiB of HBM per device.

```python
import jax
import jax.numpy as jnp
from jax import lax

D = 4096
HEADS = 16
KV_HEADS = 4
HEAD_DIM = 128
LAT_DEV = 128
SEQS = 16
LATENTS = 8192
N_CTX = 64


def draw_queries(key, part):
    shape = (SEQS, LATENTS, HEADS * HEAD_DIM)
    result = jax.random.normal(key, shape, jnp.float32)
    return result.astype(jnp.bfloat16)


def draw_doc_first(key, part):
    marks = jax.random.randint(key, (SEQS, LATENTS), 0, 3 * LAT_DEV)
    places = jnp.arange(LATENTS, dtype=jnp.int32)[None, :]
    starting = (marks == 0) | (places == 0) | (places == LATENTS - 1)
    return lax.cummax(jnp.where(starting, places, 0), axis=1).astype(jnp.int32)


def shard_levels(rng, extent, split, low, top_value):
    def one(axis_at, parts):
        steps = jax.random.uniform(jax.random.fold_in(jax.random.fold_in(rng, 6), axis_at), (parts,), jnp.float32, low / len(split), top_value / len(split))
        return jnp.repeat(jnp.exp(steps), extent[axis_at] // parts).reshape((-1,) + (1,) * (len(extent) - axis_at - 1))

    level = one(*split[0])
    for cut in split[1:]:
        level = level * one(*cut)
    return level


def noise(rng, shape, scale, limit, cuts=(), kind=jnp.bfloat16):
    drawn = jax.random.normal(rng, shape, jnp.float32) * scale
    if len(cuts) > 0:
        drawn = shard_levels(rng, shape, cuts, -0.22, 0.18) * drawn
    return jnp.clip(drawn, min=-limit, max=limit).astype(kind)


def setup_inputs(seed: int = 0) -> dict:
    key_of = jax.random.split(jax.random.key(seed), 7)
    return {
        "latents": noise(key_of[0], (SEQS, LATENTS, D), 1.0, 6.0, ((0, 16), (1, 64))),
        "queries": draw_queries(jax.random.fold_in(key_of[6], 71), 0),
        "values": noise(key_of[2], (SEQS, LATENTS, KV_HEADS * HEAD_DIM), 1.0, 6.0, ((0, 16), (1, 64))),
        "d_out": noise(key_of[3], (SEQS, LATENTS, HEADS * HEAD_DIM), 1.0, 6.0, ((0, 16), (1, 64))),
        "w_key": noise(key_of[4], (D, KV_HEADS * HEAD_DIM), D ** -0.5, 0.09375, ((0, 16),)),
        "doc_first": draw_doc_first(jax.random.fold_in(key_of[6], 71), 0),
    }


def attend_block(query_heads, key_heads, value_heads, grad_heads, visible, score_scale):
    query_wide = query_heads.astype(jnp.float32)
    key_wide = key_heads.astype(jnp.float32)
    value_wide = value_heads.astype(jnp.float32)
    grad_wide = grad_heads.astype(jnp.float32)
    scores = jnp.einsum('rkgd,skd->kgrs', query_wide, key_wide) * score_scale
    scores = jnp.where(visible, scores, -jnp.inf)
    row_top = jnp.max(scores, axis=-1, keepdims=True)
    weights = jnp.exp(scores - row_top)
    probs = weights / jnp.sum(weights, axis=-1, keepdims=True)
    probs_low = probs.astype(jnp.bfloat16).astype(jnp.float32)
    attended = jnp.einsum('kgrs,skd->rkgd', probs_low, value_wide).astype(jnp.bfloat16)
    grad_probs = jnp.einsum('rkgd,skd->kgrs', grad_wide, value_wide)
    row_delta = jnp.sum(grad_wide * attended.astype(jnp.float32), axis=-1)
    row_delta = jnp.transpose(row_delta, (1, 2, 0))[..., None]
    grad_scores = (probs * (grad_probs - row_delta) * score_scale).astype(jnp.bfloat16).astype(jnp.float32)
    grad_query = jnp.einsum('kgrs,skd->rkgd', grad_scores, key_wide).astype(jnp.bfloat16)
    grad_keys = jnp.einsum('kgrs,rkgd->skd', grad_scores, query_wide)
    grad_values = jnp.einsum('kgrs,rkgd->skd', probs_low, grad_wide)
    return attended, grad_query, grad_keys, grad_values


def pair_blocks(blocks):
    padding = jnp.zeros_like(blocks[:1])
    earlier = jnp.concatenate([padding, blocks[:-1]], axis=0)
    return jnp.concatenate([earlier, blocks], axis=1)


def combine_parts(pair_grads):
    own_part = pair_grads[:, LAT_DEV:]
    back_part = pair_grads[:, :LAT_DEV].astype(jnp.bfloat16)
    incoming = jnp.concatenate([back_part[1:], jnp.zeros_like(back_part[:1])], axis=0)
    return (own_part + incoming.astype(jnp.float32)).astype(jnp.bfloat16)


def reference(latents, queries, values, d_out, w_key, doc_first):
    groups = HEADS // KV_HEADS
    kv_width = KV_HEADS * HEAD_DIM
    score_scale = HEAD_DIM ** -0.5
    block_start = jnp.arange(N_CTX, dtype=jnp.int32)[:, None] * LAT_DEV
    query_place = block_start + jnp.arange(LAT_DEV, dtype=jnp.int32)[None, :]
    key_place = block_start - LAT_DEV + jnp.arange(2 * LAT_DEV, dtype=jnp.int32)[None, :]

    def one_sequence(total, pieces):
        tokens, query, value, grad, first = pieces
        keys = jnp.dot(tokens, w_key, preferred_element_type=jnp.float32).astype(jnp.bfloat16)
        key_pairs = pair_blocks(keys.reshape(N_CTX, LAT_DEV, KV_HEADS, HEAD_DIM))
        value_pairs = pair_blocks(value.reshape(N_CTX, LAT_DEV, KV_HEADS, HEAD_DIM))
        query_heads = query.reshape(N_CTX, LAT_DEV, KV_HEADS, groups, HEAD_DIM)
        grad_heads = grad.reshape(N_CTX, LAT_DEV, KV_HEADS, groups, HEAD_DIM)
        first_blocks = first.reshape(N_CTX, LAT_DEV)
        visible = (key_place[:, None, :] <= query_place[:, :, None]) & (key_place[:, None, :] >= first_blocks[:, :, None])
        attended, grad_query, grad_keys, grad_values = jax.vmap(attend_block, in_axes=(0, 0, 0, 0, 0, None))(
            query_heads, key_pairs, value_pairs, grad_heads, visible, score_scale)
        grad_key = combine_parts(grad_keys).reshape(N_CTX, LAT_DEV, kv_width)
        grad_value = combine_parts(grad_values).reshape(LATENTS, kv_width)
        term = jnp.einsum('crd,crk->cdk', tokens.reshape(N_CTX, LAT_DEV, D).astype(jnp.float32),
                          grad_key.astype(jnp.float32)).astype(jnp.bfloat16)
        total = total + jnp.sum(term.astype(jnp.float32), axis=0)
        return total, (attended.reshape(LATENTS, HEADS * HEAD_DIM), grad_query.reshape(LATENTS, HEADS * HEAD_DIM), grad_value)

    start_total = jnp.zeros((D, kv_width), jnp.float32)
    grad_weight, outputs = lax.scan(one_sequence, start_total, (latents, queries, values, d_out, doc_first))
    attended, grad_query, grad_value = outputs
    return attended, grad_query, grad_value, grad_weight
```

```python
import jax
import jax.numpy as jnp
from jax import lax
from jax.experimental import pallas as pl
from jax.experimental.pallas import tpu as pltpu
from jax.sharding import Mesh, PartitionSpec as P

HEADS = 16
KV_HEADS = 4
GROUPS = HEADS // KV_HEADS
HEAD_DIM = 128
ROWS = 128
AXES = ("ylo", "z", "core", "yhi", "x")
CTX = ("ylo", "z", "core")


def exchange(parts, axis):
    return lax.all_to_all(parts, axis, 0, 0, tiled=True)


def gather(part, axis):
    return exchange(jnp.broadcast_to(part[None], (lax.axis_size(axis),) + part.shape), axis)


def shift(shard, axis, by):
    count = lax.axis_size(axis)
    return lax.ppermute(shard, axis, [(i, i + by) for i in range(count) if 0 <= i + by < count])


def swap(shard):
    return lax.ppermute(shard, "core", [(0, 1), (1, 0)])


def dot(a, b, contract):
    return lax.dot_general(a, b, ((contract[:1], contract[1:]), ((), ())), preferred_element_type=jnp.float32)


def attend_kernel(place_ref, first_ref, q_ref, g_ref, kp_ref, ko_ref, vp_ref, vo_ref, att_ref, gq_ref, gk_ref, gv_ref):
    scale = HEAD_DIM ** -0.5
    start = place_ref[0]
    row = start + lax.broadcasted_iota(jnp.int32, (ROWS, 2 * ROWS), 0)
    col = start - ROWS + lax.broadcasted_iota(jnp.int32, (ROWS, 2 * ROWS), 1)
    seen = (col <= row) & (col >= first_ref[...])
    bias = jnp.where(seen, 0.0, -jnp.inf)
    bias = jnp.concatenate([bias] * GROUPS, axis=0)
    for k in range(KV_HEADS):
        kv = slice(k * HEAD_DIM, (k + 1) * HEAD_DIM)
        heads = [slice((k * GROUPS + g) * HEAD_DIM, (k * GROUPS + g + 1) * HEAD_DIM) for g in range(GROUPS)]
        q = jnp.concatenate([q_ref[:, h] for h in heads], axis=0)
        g = jnp.concatenate([g_ref[:, h] for h in heads], axis=0)
        keys = jnp.concatenate([kp_ref[:, kv], ko_ref[:, kv]], axis=0)
        values = jnp.concatenate([vp_ref[:, kv], vo_ref[:, kv]], axis=0)
        s = dot(q, keys, (1, 1)) * scale + bias
        w = jnp.exp(s - jnp.max(s, axis=1, keepdims=True))
        p = w / jnp.sum(w, axis=1, keepdims=True)
        low = p.astype(jnp.bfloat16)
        att = dot(low, values, (1, 0)).astype(jnp.bfloat16)
        delta = jnp.sum(g.astype(jnp.float32) * att.astype(jnp.float32), axis=1, keepdims=True)
        ds = (p * (dot(g, values, (1, 1)) - delta) * scale).astype(jnp.bfloat16)
        gq = dot(ds, keys, (1, 0)).astype(jnp.bfloat16)
        for i, h in enumerate(heads):
            rows = slice(i * ROWS, (i + 1) * ROWS)
            att_ref[:, h] = att[rows]
            gq_ref[:, h] = gq[rows]
        gk_ref[:, kv] = dot(ds, q, (0, 0))
        gv_ref[:, kv] = dot(low, g, (0, 0))


def attend(place, first, q, g, kp, ko, vp, vo):
    width = KV_HEADS * HEAD_DIM
    vmem = pl.BlockSpec(memory_space=pltpu.VMEM)
    return pl.pallas_call(
        attend_kernel,
        out_shape=(
            jax.ShapeDtypeStruct(q.shape, jnp.bfloat16),
            jax.ShapeDtypeStruct(q.shape, jnp.bfloat16),
            jax.ShapeDtypeStruct((2 * ROWS, width), jnp.float32),
            jax.ShapeDtypeStruct((2 * ROWS, width), jnp.float32),
        ),
        in_specs=[pl.BlockSpec(memory_space=pltpu.SMEM)] + [vmem] * 7,
        out_specs=[vmem] * 4,
        compiler_params=pltpu.CompilerParams(vmem_limit_bytes=32 << 20),
        cost_estimate=pl.CostEstimate(flops=700_000_000, bytes_accessed=4_000_000, transcendentals=600_000),
    )(place, first, q, g, kp, ko, vp, vo)


def body(latents, queries, values, d_out, w_key, doc_first):
    lat = latents[0]
    val = values[0]
    core = lax.axis_index("core")
    width = KV_HEADS * HEAD_DIM
    half = width // 2

    w_half = lax.dynamic_slice_in_dim(w_key, core * half, half, 1)
    w_y = gather(w_half, "yhi").reshape(4, 256, half)
    w_x = gather(w_y, "x").reshape(4, 4, 256, half)
    w_o = swap(w_x)

    lat_prev = shift(lat, CTX, 1)
    val_prev = shift(val, CTX, 1)
    lat_cols = lat.reshape(ROWS, 4, 4, 256).transpose(2, 0, 1, 3).reshape(4, ROWS, 1024)
    lat_x = exchange(lat_cols, "x").reshape(4 * ROWS, 1024)
    lat_o = swap(lat_x)

    both = jnp.concatenate([lat_prev, lat], axis=0).reshape(2 * ROWS, 4, 4, 256)

    def project(w):
        return jnp.einsum("tyxk,xykn->tn", both, w, preferred_element_type=jnp.float32).astype(jnp.bfloat16)

    k_mine, k_other = project(w_x), project(w_o)
    first_half = jnp.where(core == 0, k_mine, k_other)
    second_half = jnp.where(core == 0, k_other, k_mine)
    keys = jnp.concatenate([first_half, second_half], axis=1)

    place = (lax.axis_index(CTX) * ROWS).astype(jnp.int32).reshape(1)
    att, gq, gk, gv = attend(
        place, doc_first.reshape(ROWS, 1), queries[0], d_out[0], keys[:ROWS], keys[ROWS:], val_prev, val
    )
    back = jnp.concatenate([gk[:ROWS], gv[:ROWS]], axis=1).astype(jnp.bfloat16)
    ahead = shift(back, CTX, -1).astype(jnp.float32)
    grad_key = (gk[ROWS:] + ahead[:, :width]).astype(jnp.bfloat16)
    grad_value = (gv[ROWS:] + ahead[:, width:]).astype(jnp.bfloat16)

    halves = grad_key.reshape(ROWS, 2, half).transpose(1, 0, 2)
    sent = jnp.broadcast_to(halves[:, None], (2, 4, ROWS, half)).reshape(8, ROWS, half)
    got = exchange(sent, ("core", "x")).reshape(2, 4 * ROWS, half)
    g_mine = jnp.where(core == 0, got[0], got[1])
    g_other = jnp.where(core == 0, got[1], got[0])
    part = (dot(lat_x, g_mine, (0, 0)) + dot(lat_o, g_other, (0, 0))).astype(jnp.bfloat16)

    part = exchange(part.reshape(8, 128, half), ("yhi", "ylo")).reshape(8, 128, half)
    part = jnp.sum(part.astype(jnp.float32), axis=0).astype(jnp.bfloat16)
    part = exchange(part.reshape(16, 8, half), "z").reshape(16, 8, half)
    part = jnp.sum(part.astype(jnp.float32), axis=0).astype(jnp.bfloat16)
    mine = gather(part, ("ylo", "z")).reshape(256, half)
    other = swap(mine)
    left = jnp.where(core == 0, mine, other)
    right = jnp.where(core == 0, other, mine)
    grad_weight = jnp.concatenate([left, right], axis=1).astype(jnp.float32)
    return att[None], gq[None], grad_value[None], grad_weight


def solution(mesh):
    fine = Mesh(mesh.devices.reshape(2, 16, 2, 4, 4), AXES)
    row, col = ("yhi", "x"), CTX
    block = P(row, col, None)
    return jax.shard_map(
        body,
        mesh=fine,
        in_specs=(block, block, block, block, P(row, None), P(row, col)),
        out_specs=(block, block, block, P(row, None)),
        check_vma=False,
    )
```
